32 devices in a mesh: row: 4 (over z), col: 8 (over y, x, core).
Axes of the slice: x: 2, y: 2, z: 4, core: 2. Of those that a mesh axis runs over, the one named last changes fastest.
Arguments:
- block_input_rows: bfloat16 [4096, 2048], P('row', 'col'), may hold values from -40 to 40
- attention_norm_gain: float32 [2048], replicated, may hold values from 0.5 to 1.5
- query_weight: bfloat16 [2048, 2048], P('row', 'col'), may hold values from -1 to 1
- key_weight: bfloat16 [2048, 2048], P('row', 'col'), may hold values from -16 to 16
- value_weight: bfloat16 [2048, 2048], P('row', 'col'), may hold values from -0.125 to 0.125
- output_weight: bfloat16 [2048, 2048], P('col', 'row'), may hold values from -2 to 2
- feedforward_norm_gain: float32 [2048], replicated, may hold values from 0.5 to 1.5
- gate_weight: bfloat16 [2048, 8192], P('row', 'col'), may hold values from -0.125 to 0.125
- up_weight: bfloat16 [2048, 8192], P('row', 'col'), may hold values from -0.125 to 0.125
- down_weight: bfloat16 [8192, 2048], P('col', 'row'), may hold values from -0.0625 to 0.0625
- segment_ids: int32 [4096], P('row'), may hold values from 0 to 7, as said below
- positions: int32 [4096], P('row'), may hold values from 0 to 999, as said below
- output_grad: bfloat16 [4096, 2048], P('row', 'col'), may hold values from -12 to 12
Outputs:
- block_output: bfloat16 [4096, 2048], P('row', 'col')
- block_input_gradient: float32 [4096, 2048], P('row', 'col')
- query_weight_grad: float32 [2048, 2048], P('row', 'col')
- key_weight_grad: float32 [2048, 2048], P('row', 'col')
- value_weight_grad: float32 [2048, 2048], P('row', 'col')
- output_weight_grad: float32 [2048, 2048], P('col', 'row')
- attention_gain_grad: float32 [2048], P('col')
- gate_weight_grad: float32 [2048, 8192], P('row', 'col')
- up_weight_grad: float32 [2048, 8192], P('row', 'col')
- down_weight_grad: float32 [8192, 2048], P('col', 'row')
- feedforward_gain_grad: float32 [2048], P('col')
The draws below stay inside these ranges and needn't reach their ends.
Inputs may be any that keep to these rules, and one draw needn't show every extreme that they name: `segment_ids`: never falling along the tokens, starting at 0 and rising by one from document to document; consecutive documents of 100 to 1000 tokens, the first one of 1000, the last one cut by the end of the tokens. `positions`: each token's offset from the first token of its document.
All inputs are finite; a program needn't handle non-finite values.
Results may differ from the reference program's by a relative error of at most 0.015.
Values may be sent and summed in bfloat16 or wider, within the bound.
No kernel may reach another device: no remote copies, remote signals or barrier semaphores. Data moves between devices by JAX's collectives and lax.ppermute only.
A program may use at most 192 MiB of HBM per device.

```python
import math
import jax
import jax.numpy as jnp
from jax import lax

D = 2048
H = 32
HD = 64
FF = 8192
SEQ = 1024
QBLK = 512
TOKENS = 4096
DOC_HI = 1000
DOC_LO = 100


def draw_block_input_rows(key, part):
    noise_key, row_key, col_key = jax.random.split(key, 3)
    base = jax.random.normal(noise_key, (TOKENS, D), jnp.float32)
    rows = 10.0 ** jax.random.uniform(row_key, (TOKENS, 1), jnp.float32, -0.5, 0.5)
    ramp = (jnp.arange(D).astype(jnp.float32) / D)[None, :]
    jitter = 10.0 ** jax.random.uniform(col_key, (1, D), jnp.float32, -0.5, 0.5)
    cols = 3.0 ** (0.5 * ramp) * jitter
    return jnp.clip(base * rows * cols, -40.0, 40.0).astype(jnp.bfloat16)


def query_matrix(key):
    return jax.random.normal(jax.random.fold_in(key, 11), (D, H * HD), jnp.float32) / math.sqrt(D)


def draw_query_weight(key, part):
    return jnp.clip(query_matrix(key), -1.0, 1.0).astype(jnp.bfloat16)


def draw_key_weight(key, part):
    own = jax.random.normal(jax.random.fold_in(key, 12), (D, H * HD), jnp.float32) / math.sqrt(D)
    return jnp.clip(own, -16.0, 16.0).astype(jnp.bfloat16)


def doc_layout(key):
    pair_total = DOC_LO + DOC_HI
    pair_count = (TOKENS - 1) // pair_total + 1
    firsts = jax.random.randint(jax.random.fold_in(key, 21), (pair_count,), DOC_LO, DOC_HI + 1).astype(jnp.int32)
    firsts = firsts.at[0].set(DOC_HI)
    firsts = firsts.at[pair_count - 1].set(DOC_LO)
    lengths = jnp.stack([firsts, pair_total - firsts], axis=1).reshape(2 * pair_count)
    ends = jnp.cumsum(lengths).astype(jnp.int32)
    starts = ends - lengths
    token_idx = jnp.arange(TOKENS, dtype=jnp.int32)
    segment = jnp.searchsorted(ends, token_idx, side='right').astype(jnp.int32)
    offsets = (token_idx - starts[segment]).astype(jnp.int32)
    return (segment, offsets)


def draw_segment_ids(key, part):
    return doc_layout(key)[0]


def draw_positions(key, part):
    return doc_layout(key)[1]


def draw_output_grad(key, part):
    noise = jax.random.normal(jax.random.fold_in(key, 31), (TOKENS, D), jnp.float32)
    ramp = 3.0 ** (jnp.arange(TOKENS).astype(jnp.float32) / TOKENS)[:, None]
    return jnp.clip(0.6 * noise * ramp, -12.0, 12.0).astype(jnp.bfloat16)


def block_scale(key, shape, cuts, least, top_value):
    def one(axis_at, shards_of):
        draws = jax.random.uniform(jax.random.fold_in(jax.random.fold_in(key, 6), axis_at), (shards_of,), jnp.float32, least / len(cuts), top_value / len(cuts))
        return jnp.repeat(jnp.exp(draws), shape[axis_at] // shards_of).reshape((-1,) + (1,) * (len(shape) - axis_at - 1))

    gain = one(*cuts[0])
    for cut in cuts[1:]:
        gain = gain * one(*cut)
    return gain


def scatter_about(stream_key, extent, scale, limit, shards=(), held_as=jnp.bfloat16):
    factor_of = block_scale(stream_key, extent, shards, -0.22, 0.18) if shards else 1.0
    result = jax.random.normal(stream_key, extent, jnp.float32) * scale * factor_of
    return jnp.minimum(jnp.maximum(result, -limit), limit).astype(held_as)


def setup_inputs(seed: int = 0) -> dict:
    arg_keys = jax.random.split(jax.random.key(seed), 14)
    return {
        "block_input_rows": draw_block_input_rows(jax.random.fold_in(arg_keys[13], 71), 0),
        "attention_norm_gain": jnp.clip(1.0 + 0.1 * jax.random.normal(arg_keys[1], (D,), jnp.float32), 0.5, 1.5),
        "query_weight": draw_query_weight(jax.random.fold_in(arg_keys[13], 71), 0),
        "key_weight": draw_key_weight(jax.random.fold_in(arg_keys[13], 71), 0),
        "value_weight": scatter_about(arg_keys[4], (D, H * HD), D ** -0.5, 0.125, ((0, 4), (1, 8))),
        "output_weight": scatter_about(arg_keys[5], (H * HD, D), (max(1, H * HD // 256)) ** -0.5, 2.0, ((0, 8), (1, 4))),
        "feedforward_norm_gain": jnp.clip(1.0 + 0.1 * jax.random.normal(arg_keys[6], (D,), jnp.float32), 0.5, 1.5),
        "gate_weight": scatter_about(arg_keys[7], (D, FF), D ** -0.5, 0.125, ((0, 4), (1, 8))),
        "up_weight": scatter_about(arg_keys[8], (D, FF), D ** -0.5, 0.125, ((0, 4), (1, 8))),
        "down_weight": scatter_about(arg_keys[9], (FF, D), FF ** -0.5, 0.0625, ((0, 8), (1, 4))),
        "segment_ids": draw_segment_ids(jax.random.fold_in(arg_keys[13], 71), 0),
        "positions": draw_positions(jax.random.fold_in(arg_keys[13], 71), 0),
        "output_grad": draw_output_grad(jax.random.fold_in(arg_keys[13], 71), 0),
    }


EPS = 1e-05
THETA = 130000.0
NEG = -1e+30

def round_to_brain_float(values):
    return lax.optimization_barrier(values.astype(jnp.bfloat16))

def rope_tables(places, head_size):
    half_size = head_size // 2
    freq = jnp.exp(-(2.0 * jnp.arange(half_size).astype(jnp.float32) / head_size) * math.log(THETA))
    angle = places.astype(jnp.float32)[:, None] * freq[None, :]
    return (jnp.cos(angle)[:, None, :], jnp.sin(angle)[:, None, :])

def rotate(values, cosine, sine):
    half_size = values.shape[-1] // 2
    front_half = values[..., :half_size]
    back_half = values[..., half_size:]
    return jnp.concatenate([front_half * cosine - back_half * sine, back_half * cosine + front_half * sine], axis=-1)

def unrotate(values, cosine, sine):
    half_size = values.shape[-1] // 2
    front_half = values[..., :half_size]
    back_half = values[..., half_size:]
    return jnp.concatenate([front_half * cosine + back_half * sine, back_half * cosine - front_half * sine], axis=-1)

def masked_scores(query_f, key_f, segments, lower, scale):
    block_query = query_f[lower:lower + QBLK]
    scores = jnp.einsum('qhd,khd->hqk', block_query, key_f) * scale
    query_pos = lower + jnp.arange(QBLK)
    key_pos = jnp.arange(SEQ)
    allowed = (key_pos[None, :] <= query_pos[:, None]) & (segments[None, :] == segments[lower:lower + QBLK, None])
    return (jnp.where(allowed[None], scores, NEG), block_query)

def attend(query, key, value, segments, scale):
    query_f = query.astype(jnp.float32)
    key_f = key.astype(jnp.float32)
    value_f = value.astype(jnp.float32)
    outputs = []
    lse_parts = []
    for block_num in range(SEQ // QBLK):
        scores, block_query = masked_scores(query_f, key_f, segments, block_num * QBLK, scale)
        top = lax.optimization_barrier(jnp.max(scores, axis=-1, keepdims=True))
        lse = top + jnp.log(lax.optimization_barrier(jnp.sum(jnp.exp(scores - top), axis=-1, keepdims=True)))
        probs = round_to_brain_float(jnp.exp(scores - lse))
        outputs.append(round_to_brain_float(jnp.einsum('hqk,khd->qhd', probs.astype(jnp.float32), value_f)))
        lse_parts.append(lse)
    return (jnp.concatenate(outputs, axis=0), jnp.concatenate(lse_parts, axis=1))

def attend_back(query, key, value, segments, outputs, lse_all, dout, scale):
    query_f = query.astype(jnp.float32)
    key_f = key.astype(jnp.float32)
    value_f = value.astype(jnp.float32)
    dout_f = dout.astype(jnp.float32)
    delta = jnp.transpose(lax.optimization_barrier(jnp.sum(dout_f * outputs.astype(jnp.float32), axis=-1)))
    dkey = jnp.zeros(key.shape, jnp.float32)
    dvalue = jnp.zeros(value.shape, jnp.float32)
    dquery_parts = []
    for block_num in range(SEQ // QBLK):
        lower = block_num * QBLK
        scores, block_query = masked_scores(query_f, key_f, segments, lower, scale)
        probs = jnp.exp(scores - lse_all[:, lower:lower + QBLK])
        probs_b = round_to_brain_float(probs).astype(jnp.float32)
        block_dout = dout_f[lower:lower + QBLK]
        dvalue = dvalue + jnp.einsum('hqk,qhd->khd', probs_b, block_dout)
        dprob = jnp.einsum('qhd,khd->hqk', block_dout, value_f)
        dscore = round_to_brain_float(probs * (dprob - delta[:, lower:lower + QBLK, None])).astype(jnp.float32)
        dquery_parts.append(jnp.einsum('hqk,khd->qhd', dscore, key_f) * scale)
        dkey = dkey + jnp.einsum('hqk,qhd->khd', dscore, block_query) * scale
    return (jnp.concatenate(dquery_parts, axis=0), dkey, dvalue)

def mm(left, right):
    return jnp.dot(left, right, preferred_element_type=jnp.float32)

def reference(block_input_rows, attention_norm_gain, query_weight, key_weight, value_weight, output_weight, feedforward_norm_gain, gate_weight, up_weight, down_weight, segment_ids, positions, output_grad):
    scale = 1.0 / math.sqrt(HD)
    seq_count = TOKENS // SEQ

    def one_sequence(totals, item):
        tokens, segments, places, upstream_gradient = item
        input_wide_float = tokens.astype(jnp.float32)
        first_inverse_deviation = lax.rsqrt(lax.optimization_barrier(jnp.mean(input_wide_float * input_wide_float, axis=-1, keepdims=True)) + EPS)
        first_centered_unit = input_wide_float * first_inverse_deviation
        first_normalized = round_to_brain_float(first_centered_unit * attention_norm_gain)
        cosine, sine = rope_tables(places, HD)
        query = round_to_brain_float(rotate(mm(first_normalized, query_weight).reshape(SEQ, H, HD), cosine, sine))
        key = round_to_brain_float(rotate(mm(first_normalized, key_weight).reshape(SEQ, H, HD), cosine, sine))
        value = round_to_brain_float(mm(first_normalized, value_weight).reshape(SEQ, H, HD))
        attended, lse_all = attend(query, key, value, segments, scale)
        attended_flat = attended.reshape(SEQ, H * HD)
        middle_residual = input_wide_float + mm(attended_flat, output_weight)
        second_inverse_deviation = lax.rsqrt(lax.optimization_barrier(jnp.mean(middle_residual * middle_residual, axis=-1, keepdims=True)) + EPS)
        second_centered_unit = middle_residual * second_inverse_deviation
        second_normalized = round_to_brain_float(second_centered_unit * feedforward_norm_gain)
        gate = mm(second_normalized, gate_weight)
        up_proj = mm(second_normalized, up_weight)
        sigm = jax.nn.sigmoid(gate)
        silu_gate = gate * sigm
        hidden = round_to_brain_float(silu_gate * up_proj)
        block_out = (middle_residual + mm(hidden, down_weight)).astype(jnp.bfloat16)
        dhidden = mm(upstream_gradient, down_weight.T)
        grad_down = mm(hidden.T, upstream_gradient)
        dgate = round_to_brain_float(dhidden * up_proj * sigm * (1.0 + gate * (1.0 - sigm)))
        dup = round_to_brain_float(dhidden * silu_gate)
        grad_gate = mm(second_normalized.T, dgate)
        grad_up = mm(second_normalized.T, dup)
        second_normalized_gradient = mm(dgate, gate_weight.T) + mm(dup, up_weight.T)
        feedforward_gain_partial = lax.optimization_barrier(jnp.sum(second_normalized_gradient * second_centered_unit, axis=0))
        second_scaled_rows = feedforward_norm_gain * second_normalized_gradient
        middle_gradient = upstream_gradient.astype(jnp.float32) + second_inverse_deviation * (second_scaled_rows - second_centered_unit * lax.optimization_barrier(jnp.mean(second_scaled_rows * second_centered_unit, axis=-1, keepdims=True)))
        dmiddle_b = round_to_brain_float(middle_gradient)
        dattended = round_to_brain_float(mm(dmiddle_b, output_weight.T)).reshape(SEQ, H, HD)
        grad_output = mm(attended_flat.T, dmiddle_b)
        dquery_rot, dkey_rot, dvalue_f = attend_back(query, key, value, segments, attended, lse_all, dattended, scale)
        dquery = round_to_brain_float(unrotate(dquery_rot, cosine, sine)).reshape(SEQ, H * HD)
        dkey = round_to_brain_float(unrotate(dkey_rot, cosine, sine)).reshape(SEQ, H * HD)
        dvalue = round_to_brain_float(dvalue_f).reshape(SEQ, H * HD)
        grad_query = mm(first_normalized.T, dquery)
        grad_key = mm(first_normalized.T, dkey)
        grad_value = mm(first_normalized.T, dvalue)
        first_normalized_gradient = mm(dquery, query_weight.T) + mm(dkey, key_weight.T) + mm(dvalue, value_weight.T)
        attention_gain_partial = lax.optimization_barrier(jnp.sum(first_normalized_gradient * first_centered_unit, axis=0))
        first_scaled_rows = attention_norm_gain * first_normalized_gradient
        input_gradient = middle_gradient + first_inverse_deviation * (first_scaled_rows - first_centered_unit * lax.optimization_barrier(jnp.mean(first_scaled_rows * first_centered_unit, axis=-1, keepdims=True)))
        terms = (grad_query, grad_key, grad_value, grad_output, attention_gain_partial, grad_gate, grad_up, grad_down, feedforward_gain_partial)
        totals = tuple((total + term for total, term in zip(totals, terms)))
        return (totals, (block_out, input_gradient))
    initial = (jnp.zeros((D, H * HD), jnp.float32), jnp.zeros((D, H * HD), jnp.float32), jnp.zeros((D, H * HD), jnp.float32), jnp.zeros((H * HD, D), jnp.float32), jnp.zeros((D,), jnp.float32), jnp.zeros((D, FF), jnp.float32), jnp.zeros((D, FF), jnp.float32), jnp.zeros((FF, D), jnp.float32), jnp.zeros((D,), jnp.float32))
    items = (block_input_rows.reshape(seq_count, SEQ, D), segment_ids.reshape(seq_count, SEQ), positions.reshape(seq_count, SEQ), output_grad.reshape(seq_count, SEQ, D))
    totals, stacked = lax.scan(one_sequence, initial, items)
    block_output = stacked[0].reshape(TOKENS, D)
    block_input_gradient = stacked[1].reshape(TOKENS, D)
    return (block_output, block_input_gradient, totals[0], totals[1], totals[2], totals[3], totals[4], totals[5], totals[6], totals[7], totals[8])
```

```python
import math

import jax
import jax.numpy as jnp
from jax import lax
from jax.sharding import PartitionSpec as P

HD = 64
SEQ = 1024
QBLK = 512
CHUNKS = 4

EPS = 1e-05
THETA = 130000.0
NEG = -1e30


BF = jnp.bfloat16
F32 = jnp.float32


def rope_tables(places, head_size):
    half_size = head_size // 2
    freq = jnp.exp(-(2.0 * jnp.arange(half_size).astype(F32) / head_size) * math.log(THETA))
    angle = places.astype(F32)[:, None] * freq[None, :]
    return (jnp.cos(angle)[:, None, :], jnp.sin(angle)[:, None, :])


def rotate(values, cosine, sine):
    half_size = values.shape[-1] // 2
    front_half = values[..., :half_size]
    back_half = values[..., half_size:]
    return jnp.concatenate(
        [front_half * cosine - back_half * sine, back_half * cosine + front_half * sine], axis=-1
    )


def unrotate(values, cosine, sine):
    half_size = values.shape[-1] // 2
    front_half = values[..., :half_size]
    back_half = values[..., half_size:]
    return jnp.concatenate(
        [front_half * cosine + back_half * sine, back_half * cosine - front_half * sine], axis=-1
    )


def matmul(left, right):
    return jnp.dot(left, right, preferred_element_type=F32)


def matmul_nt(left, right):
    return lax.dot_general(left, right, (((1,), (1,)), ((), ())), preferred_element_type=F32)


def matmul_tn(left, right):
    return lax.dot_general(left, right, (((0,), (0,)), ((), ())), preferred_element_type=F32)


def after(values, *deps):
    return lax.optimization_barrier((values, deps))[0]


def block_scores(query, key, segments, lower, upper, scale):
    block_query = query[:, lower : lower + QBLK]
    scores = (
        jnp.einsum("sqhd,skhd->shqk", block_query, key[:, :upper], preferred_element_type=F32)
        * scale
    )
    query_pos = lower + jnp.arange(QBLK)
    key_pos = jnp.arange(upper)
    causal = key_pos[None, :] <= query_pos[:, None]
    same_doc = segments[:, lower : lower + QBLK, None] == segments[:, None, :upper]
    allowed = (causal[None] & same_doc)[:, None]
    return (jnp.where(allowed, scores, NEG), block_query)


def attend(query, key, value, segments, scale):
    outputs = []
    lse_parts = []
    for block_num in range(SEQ // QBLK):
        lower = block_num * QBLK
        upper = lower + QBLK
        scores, block_query = block_scores(query, key, segments, lower, upper, scale)
        top = jnp.max(scores, axis=-1, keepdims=True)
        lse = top + jnp.log(jnp.sum(jnp.exp(scores - top), axis=-1, keepdims=True))
        probs = jnp.exp(scores - lse).astype(BF)
        outputs.append(
            jnp.einsum(
                "shqk,skhd->sqhd", probs, value[:, :upper], preferred_element_type=F32
            ).astype(BF)
        )
        lse_parts.append(lse)
    return (jnp.concatenate(outputs, axis=1), jnp.concatenate(lse_parts, axis=2))


def attend_back(query, key, value, segments, outputs, lse_all, dout, scale):
    delta = jnp.transpose(
        jnp.sum(dout.astype(F32) * outputs.astype(F32), axis=-1), (0, 2, 1)
    )[..., None]
    dkey = jnp.zeros(key.shape, F32)
    dvalue = jnp.zeros(value.shape, F32)
    dquery_parts = []
    for block_num in range(SEQ // QBLK):
        lower = block_num * QBLK
        upper = lower + QBLK
        scores, block_query = block_scores(query, key, segments, lower, upper, scale)
        probs = jnp.exp(scores - lse_all[:, :, lower:upper])
        probs_b = probs.astype(BF)
        block_dout = dout[:, lower:upper]
        dvalue = dvalue.at[:, :upper].add(
            jnp.einsum("shqk,sqhd->skhd", probs_b, block_dout, preferred_element_type=F32)
        )
        dprob = jnp.einsum(
            "sqhd,skhd->shqk", block_dout, value[:, :upper], preferred_element_type=F32
        )
        dscore = (probs * (dprob - delta[:, :, lower:upper])).astype(BF)
        dquery_parts.append(
            jnp.einsum("shqk,skhd->sqhd", dscore, key[:, :upper], preferred_element_type=F32)
            * scale
        )
        dkey = dkey.at[:, :upper].add(
            jnp.einsum("shqk,sqhd->skhd", dscore, block_query, preferred_element_type=F32) * scale
        )
    return (jnp.concatenate(dquery_parts, axis=1), dkey, dvalue)


class RowChain:
    def __init__(self, depth):
        self.count = lax.axis_size("row")
        self.up = [(i, i + 1) for i in range(self.count - 1)]
        self.down = [(i + 1, i) for i in range(self.count - 1)]
        self.depth = depth
        self.sent = []

    def step(self, rising, falling, queued=True):
        if queued and len(self.sent) >= self.depth:
            rising, falling = after((rising, falling), self.sent[-self.depth])
        got = (lax.ppermute(rising, "row", self.up), lax.ppermute(falling, "row", self.down))
        if queued:
            self.sent.append(got)
        return got

    def gather(self, units):
        rising = [[unit] for unit in units]
        falling = [[unit] for unit in units]
        for _ in range(1, self.count):
            for index in range(len(units)):
                got = self.step(rising[index][-1], falling[index][-1])
                rising[index].append(got[0])
                falling[index].append(got[1])
        return [
            jnp.concatenate(
                [unit]
                + [falling[index][k] + rising[index][self.count - k] for k in range(1, self.count)],
                axis=0,
            )
            for index, unit in enumerate(units)
        ]

    def reduce(self, parts):
        count = self.count
        rising, falling = parts(count - 1), parts(1)
        for step in range(1, count):
            got_rising = lax.ppermute(rising, "row", self.up)
            got_falling = lax.ppermute(falling, "row", self.down)
            if step < count - 1:
                rising = parts(count - 1 - step) + got_rising
                falling = parts(step + 1) + got_falling
        return parts(0).astype(F32) + got_rising.astype(F32) + got_falling.astype(F32)


def local(
    block_input_rows,
    attention_norm_gain,
    query_weight,
    key_weight,
    value_weight,
    output_weight,
    feedforward_norm_gain,
    gate_weight,
    up_weight,
    down_weight,
    segment_ids,
    positions,
    output_grad,
):
    col_count = lax.axis_size("col")
    row_count = lax.axis_size("row")
    col_index = lax.axis_index("col")
    row_index = lax.axis_index("row")
    tok_rows, local_width = block_input_rows.shape
    width = local_width * col_count
    row_block = query_weight.shape[0]
    head_width = query_weight.shape[1]
    heads_here = head_width // HD
    hidden_here = gate_weight.shape[1]
    piece = hidden_here // CHUNKS
    own_tokens = tok_rows // col_count
    token_begin = col_index * own_tokens
    shift = row_index * row_block
    own_place = (col_index * local_width - shift) % width
    seq_count = tok_rows // SEQ
    scale = 1.0 / math.sqrt(HD)

    def roll(values, axis=-1):
        return lax.dynamic_slice_in_dim(
            jnp.concatenate([values, values], axis=axis), shift, width, axis
        )

    def unroll(values, axis=-1):
        return lax.dynamic_slice_in_dim(
            jnp.concatenate([values, values], axis=axis), (width - shift) % width, width, axis
        )

    chain = RowChain(2)
    attn_units = chain.gather(
        [
            jnp.concatenate([query_weight, key_weight], axis=1),
            jnp.concatenate([value_weight, output_weight.T], axis=1),
        ]
    )
    down_t = down_weight.T
    ffn_units = []
    for first in range(0, CHUNKS, 2):
        ffn_units += chain.gather(
            [
                jnp.concatenate(
                    [
                        part[:, index * piece : (index + 1) * piece]
                        for part in (gate_weight, up_weight, down_t)
                    ],
                    axis=1,
                )
                for index in range(first, min(first + 2, CHUNKS))
            ]
        )
    whole_qk = attn_units[0]
    whole_value = attn_units[1][:, :head_width]
    whole_output_t = attn_units[1][:, head_width:]

    inputs_full = roll(lax.all_gather(block_input_rows, "col", axis=1, tiled=True))
    grad_full = roll(
        lax.all_gather(after(output_grad, inputs_full), "col", axis=1, tiled=True)
    )
    attn_gain = roll(attention_norm_gain)
    ffn_gain = roll(feedforward_norm_gain)

    inputs_f32 = inputs_full.astype(F32)
    input_inverse_deviation = lax.rsqrt(
        jnp.mean(inputs_f32 * inputs_f32, axis=-1, keepdims=True) + EPS
    )
    normed_in = (inputs_f32 * input_inverse_deviation * attn_gain).astype(BF)
    cosine, sine = rope_tables(positions, HD)
    query_key = matmul(normed_in, whole_qk)
    query = rotate(
        query_key[:, :head_width].reshape(tok_rows, heads_here, HD), cosine, sine
    ).astype(BF)
    key = rotate(
        query_key[:, head_width:].reshape(tok_rows, heads_here, HD), cosine, sine
    ).astype(BF)
    value = matmul(normed_in, whole_value).astype(BF)
    seq_shape = (seq_count, SEQ, heads_here, HD)
    segments = segment_ids.reshape(seq_count, SEQ)
    query_seq = query.reshape(seq_shape)
    key_seq = key.reshape(seq_shape)
    value_seq = value.reshape(seq_shape)
    attended, lse_kept = attend(query_seq, key_seq, value_seq, segments, scale)
    attended_flat = attended.reshape(tok_rows, head_width)
    out_terms = matmul_nt(attended_flat, whole_output_t).astype(BF)

    def own_rows(values):
        return lax.dynamic_slice_in_dim(values, token_begin, own_tokens, 0)

    middle_rows = own_rows(inputs_full).astype(F32) + lax.psum_scatter(
        out_terms, "col", scatter_dimension=0, tiled=True
    ).astype(F32)
    middle_full = lax.all_gather(middle_rows.astype(BF), "col", axis=0, tiled=True)
    middle_f32 = middle_full.astype(F32)
    middle_normalized = (
        middle_f32
        * lax.rsqrt(jnp.mean(middle_f32 * middle_f32, axis=-1, keepdims=True) + EPS)
        * ffn_gain
    ).astype(BF)

    dnormed_terms = None
    hidden_parts = []
    down_parts = []
    ffn_grads = []
    for index in range(CHUNKS):
        whole = ffn_units[index]
        whole_gate_up = whole[:, : 2 * piece]
        whole_down_t = whole[:, 2 * piece :]
        dhidden = matmul(grad_full, whole_down_t)
        gate_up = matmul(middle_normalized, whole_gate_up)
        gate = gate_up[:, :piece]
        up_proj = gate_up[:, piece:]
        sigm = jax.nn.sigmoid(gate)
        silu_gate = gate * sigm
        hidden = (silu_gate * up_proj).astype(BF)
        dgate = (dhidden * up_proj * sigm * (1.0 + gate * (1.0 - sigm))).astype(BF)
        dup = (dhidden * silu_gate).astype(BF)
        dgate_up = jnp.concatenate([dgate, dup], axis=1)
        terms = matmul_nt(dgate_up, whole_gate_up)
        dnormed_terms = terms if dnormed_terms is None else dnormed_terms + terms
        grad_gate_up = matmul_tn(middle_normalized, dgate_up).astype(BF)
        grad_down_t = matmul_tn(grad_full, hidden).astype(BF)

        def parts(place, grad_gate_up=grad_gate_up, grad_down_t=grad_down_t):
            begin = place * row_block
            return jnp.concatenate(
                [
                    grad_gate_up[begin : begin + row_block],
                    grad_down_t[begin : begin + row_block],
                ],
                axis=1,
            )

        ffn_grads.append(chain.reduce(parts))
        hidden_parts.append(hidden)
        down_parts.append(whole_down_t)

    dnormed_rows = lax.psum_scatter(
        dnormed_terms.astype(BF), "col", scatter_dimension=0, tiled=True
    ).astype(F32)
    middle_inverse_deviation = lax.rsqrt(
        jnp.mean(middle_rows * middle_rows, axis=-1, keepdims=True) + EPS
    )
    middle_unit = middle_rows * middle_inverse_deviation
    scaled_rows = ffn_gain * dnormed_rows
    dmiddle_rows = own_rows(grad_full).astype(F32) + middle_inverse_deviation * (
        scaled_rows - middle_unit * jnp.mean(scaled_rows * middle_unit, axis=-1, keepdims=True)
    )
    ffn_gain_terms = jnp.sum(dnormed_rows * middle_unit, axis=0)
    dmiddle_bf = lax.all_gather(dmiddle_rows.astype(BF), "col", axis=0, tiled=True)

    down_terms = matmul_nt(
        jnp.concatenate(hidden_parts, axis=1), jnp.concatenate(down_parts, axis=1)
    ).astype(BF)
    down_own = lax.psum_scatter(
        unroll(after(down_terms, dmiddle_bf)), "col", scatter_dimension=1, tiled=True
    ).astype(F32)
    block_output = (
        lax.dynamic_slice_in_dim(middle_full, own_place, local_width, 1).astype(F32) + down_own
    ).astype(BF)

    dattended = matmul(dmiddle_bf, whole_output_t).astype(BF)
    grad_output_t = matmul_tn(dmiddle_bf, attended_flat).astype(BF)
    output_grad_own = chain.reduce(
        lambda place: grad_output_t[place * row_block : (place + 1) * row_block]
    )
    dquery_rot, dkey_rot, dvalue_f = attend_back(
        query_seq,
        key_seq,
        value_seq,
        segments,
        attended,
        lse_kept,
        dattended.reshape(seq_shape),
        scale,
    )
    dquery = unrotate(dquery_rot.reshape(tok_rows, heads_here, HD), cosine, sine).astype(BF)
    dkey = unrotate(dkey_rot.reshape(tok_rows, heads_here, HD), cosine, sine).astype(BF)
    dqkv = jnp.concatenate(
        [
            dquery.reshape(tok_rows, head_width),
            dkey.reshape(tok_rows, head_width),
            dvalue_f.reshape(tok_rows, head_width).astype(BF),
        ],
        axis=1,
    )
    grad_qkv = matmul_tn(normed_in, dqkv).astype(BF)
    qkv_grad_own = chain.reduce(
        lambda place: grad_qkv[place * row_block : (place + 1) * row_block]
    )
    dinput_terms = matmul_nt(dqkv[:, : 2 * head_width], whole_qk) + matmul_nt(
        dqkv[:, 2 * head_width :], whole_value
    )
    input_unit = inputs_f32 * input_inverse_deviation
    weighted_terms = dinput_terms * input_unit
    moment_terms = jnp.sum(weighted_terms * attn_gain, axis=-1, keepdims=True)
    attn_gain_terms = jnp.sum(weighted_terms, axis=0)
    dnormed_own = lax.psum_scatter(
        unroll(dinput_terms.astype(BF)), "col", scatter_dimension=1, tiled=True
    ).astype(F32)
    input_moments = lax.psum(moment_terms, "col") / width
    gain_sums = lax.psum(unroll(jnp.stack([attn_gain_terms, ffn_gain_terms])), ("row", "col"))
    column_begin = col_index * local_width
    gain_own = lax.dynamic_slice_in_dim(gain_sums, column_begin, local_width, 1)
    attn_gain_own = lax.dynamic_slice_in_dim(attention_norm_gain, column_begin, local_width)
    block_input_gradient = lax.dynamic_slice_in_dim(
        dmiddle_bf, own_place, local_width, 1
    ).astype(F32) + input_inverse_deviation * (
        attn_gain_own * dnormed_own
        - block_input_rows.astype(F32) * input_inverse_deviation * input_moments
    )
    return (
        block_output,
        block_input_gradient,
        qkv_grad_own[:, :head_width],
        qkv_grad_own[:, head_width : 2 * head_width],
        qkv_grad_own[:, 2 * head_width :],
        output_grad_own.T,
        gain_own[0],
        jnp.concatenate([grad[:, :piece] for grad in ffn_grads], axis=1),
        jnp.concatenate([grad[:, piece : 2 * piece] for grad in ffn_grads], axis=1),
        jnp.concatenate([grad[:, 2 * piece :] for grad in ffn_grads], axis=1).T,
        gain_own[1],
    )


def solution(mesh):
    return jax.shard_map(
        local,
        mesh=mesh,
        in_specs=(
            P("row", "col"),
            P(),
            P("row", "col"),
            P("row", "col"),
            P("row", "col"),
            P("col", "row"),
            P(),
            P("row", "col"),
            P("row", "col"),
            P("col", "row"),
            P("row"),
            P("row"),
            P("row", "col"),
        ),
        out_specs=(
            P("row", "col"),
            P("row", "col"),
            P("row", "col"),
            P("row", "col"),
            P("row", "col"),
            P("col", "row"),
            P("col"),
            P("row", "col"),
            P("row", "col"),
            P("col", "row"),
            P("col"),
        ),
        check_vma=False,
    )
```
